128 devices in a mesh: segment: 4 (over z), band: 32 (over x, y, core).
Axes of the slice: x: 4, y: 4, z: 4, core: 2. Of those that a mesh axis runs over, the one named last changes fastest.
Arguments:
- clip: bfloat16 [2, 128, 160, 128], P(None, 'band'), may hold values from -6 to 6
- caches: bfloat16 [4, 4, 2, 128, 160, 128], P('segment', None, None, 'band'), may hold values from -4 to 4
- weights: bfloat16 [4, 4, 9, 3, 128, 128], P('segment'), may hold values from -0.109375 to 0.109375
- biases: float32 [4, 4, 128], P('segment'), may hold values from -2 to 2
- section_layers: int32 [4], P('segment'), may hold values from 1 to 4, as said below
Outputs:
- section_out: bfloat16 [4, 2, 128, 160, 128], P('segment', None, 'band')
The draws below stay inside these ranges and needn't reach their ends.
Inputs may be any that keep to these rules, and one draw needn't show every extreme that they name: `section_layers`: each section has 1 to 4 layers, and some section has exactly 4.
All inputs are finite; a program needn't handle non-finite values.
Results may differ from the reference program's by a relative error of at most 0.024.
Values may be sent and summed in bfloat16 or wider, within the bound.
A program may use at most 128 MiB of HBM per device.

```python
import jax
import jax.numpy as jnp

C = 128
W = 160
LMAX = 4
FRAMES = 2
SECTIONS = 4
ROWS = 128


def draw_section_layers(key, part):
    base = jax.random.randint(jax.random.fold_in(key, 11), (SECTIONS,), 1, LMAX + 1)
    chosen = jax.random.randint(jax.random.fold_in(key, 12), (), 0, SECTIONS)
    return jnp.where(jnp.arange(SECTIONS) == chosen, LMAX, base).astype(jnp.int32)


def block_levels(stream_key, dims, split, smallest, top_value):
    factor_of, own = 1.0, jax.random.fold_in(stream_key, 6)
    for dim, shards_of in split:
        steps = jnp.exp(jax.random.uniform(jax.random.fold_in(own, dim), (shards_of,), jnp.float32, smallest / len(split), top_value / len(split)))
        factor_of = factor_of * jnp.repeat(steps, dims[dim] // shards_of).reshape([-1 if axis == dim else 1 for axis in range(len(dims))])
    return factor_of


def bell_draw(rng, dims, deviation, bound, split=(), held_as=jnp.bfloat16):
    level = block_levels(rng, dims, split, -0.22, 0.18) if split else 1.0
    drawn = jax.random.normal(rng, dims, jnp.float32) * deviation * level
    return jnp.minimum(jnp.maximum(drawn, -bound), bound).astype(held_as)


def setup_inputs(seed: int = 0) -> dict:
    key_list = jax.random.split(jax.random.key(seed), 6)
    clip = bell_draw(key_list[0], (FRAMES, ROWS, W, C), 1.0, 6.0, ((1, 32),))
    caches = bell_draw(key_list[1], (SECTIONS, LMAX, 2, ROWS, W, C), 0.5, 4.0, ((0, 4), (3, 32)))
    weights = bell_draw(key_list[2], (SECTIONS, LMAX, 9, 3, C, C), (27 * C) ** -0.5, 0.109375, ((0, 4),))
    biases = bell_draw(key_list[3], (SECTIONS, LMAX, C), 0.3, 2.0, ((0, 4),), jnp.float32)
    section_layers = draw_section_layers(jax.random.fold_in(key_list[5], 71), 0)
    return dict(clip=clip, caches=caches, weights=weights, biases=biases, section_layers=section_layers)


def conv_layer(x, past, kernel, bias):
    act = jax.nn.silu(x.astype(jnp.float32)).astype(jnp.bfloat16)
    stack = jnp.concatenate([past, act[None]], axis=0)
    padded = jnp.pad(stack, ((0, 0), (1, 1), (1, 1), (0, 0)))
    rows = x.shape[0]
    width = x.shape[1]
    total = jnp.zeros(x.shape, jnp.float32)
    for k in range(9):
        row_tap = k // 3
        col_tap = k % 3
        piece = padded[:, row_tap:row_tap + rows, col_tap:col_tap + width, :]
        total = total + jnp.einsum("trwc,tcd->rwd", piece.astype(jnp.float32), kernel[k].astype(jnp.float32))
    result = (x.astype(jnp.float32) + total + bias).astype(jnp.bfloat16)
    return result, jnp.concatenate([past[1:], act[None]], axis=0)


def reference(clip, caches, weights, biases, section_layers):
    inputs = clip
    results = []
    for section in range(SECTIONS):
        history = [caches[section, layer] for layer in range(LMAX)]
        produced = []
        for frame in range(FRAMES):
            x = inputs[frame]
            for layer in range(LMAX):
                result, renewed = conv_layer(x, history[layer], weights[section, layer], biases[section, layer])
                live = layer < section_layers[section]
                x = jnp.where(live, result, x)
                history[layer] = jnp.where(live, renewed, history[layer])
            produced.append(x)
        inputs = jnp.stack(produced)
        results.append(inputs)
    return jnp.stack(results)
```

```python
import functools

import jax
import jax.numpy as jnp
from jax import lax
from jax.experimental import pallas as pl
from jax.experimental.pallas import tpu as pltpu
from jax.sharding import PartitionSpec as P

MESH = pl.DeviceIdType.MESH
PAD = 8


def kernel(dims, live_ref, bias_ref, clip, caches, weights, out, *scratch):
    segments, bands, frames, own, width, chan, depth = dims
    (wd, cext, c3, a3, sh, xs, xin, outs) = scratch[:8]
    p0 = scratch[8 : 8 + depth]
    p1 = scratch[8 + depth : 8 + 2 * depth]
    (w_sem, cl_sem, ch_send, ch_recv, cm_sem, k_send, x_send, x_recv, out_sem) = scratch[8 + 2 * depth :]
    halo = depth
    ext = own + 2 * halo
    seg = lax.axis_index("segment")
    band = lax.axis_index("band")
    first, last = seg == 0, seg == segments - 1
    has_up, has_down = band > 0, band < bands - 1

    w_copies = [
        [
            pltpu.make_async_copy(
                weights.at[0, l, :, t],
                wd.at[l, :, :, pl.ds((2 - t) * chan, chan)],
                w_sem.at[l, t],
            )
            for t in range(3)
        ]
        for l in range(depth)
    ]
    cl_copies = [
        pltpu.make_async_copy(caches.at[0, l], cext.at[l, :, pl.ds(halo, own)], cl_sem.at[l])
        for l in range(depth)
    ]
    clip_copy = pltpu.make_async_copy(clip, xin.at[:, pl.ds(halo, own)], cm_sem)
    for l in range(depth):
        cl_copies[l].start()
        for t in range(3):
            w_copies[l][t].start()

    @pl.when(first)
    def _():
        clip_copy.start()

    barrier = pltpu.get_barrier_semaphore()
    up_n, down_n = has_up.astype(jnp.int32), has_down.astype(jnp.int32)
    before, after = 1 - first.astype(jnp.int32), 1 - last.astype(jnp.int32)

    def greet(cond, ds, db):
        @pl.when(cond)
        def _():
            pl.semaphore_signal(
                barrier, inc=1, device_id={"segment": seg + ds, "band": band + db}, device_id_type=MESH
            )

    greet(has_up, 0, -1)
    greet(has_down, 0, 1)
    for ds, cond in ((-1, jnp.logical_not(first)), (1, jnp.logical_not(last))):
        greet(cond, ds, 0)
        greet(jnp.logical_and(cond, has_up), ds, -1)
        greet(jnp.logical_and(cond, has_down), ds, 1)
    pl.semaphore_wait(barrier, (up_n + down_n) * (1 + before + after) + before + after)

    def cache_down(l):
        return pltpu.make_async_remote_copy(
            caches.at[0, l, :, pl.ds(l, own - l)],
            cext.at[l, :, pl.ds(l, own - l)],
            ch_send.at[l, 0],
            ch_recv.at[l, 0],
            device_id={"segment": seg, "band": band + 1},
            device_id_type=MESH,
        )

    def cache_up(l):
        return pltpu.make_async_remote_copy(
            caches.at[0, l, :, pl.ds(0, own - l)],
            cext.at[l, :, pl.ds(halo + own, own - l)],
            ch_send.at[l, 1],
            ch_recv.at[l, 1],
            device_id={"segment": seg, "band": band - 1},
            device_id_type=MESH,
        )

    def place(k):
        return (pl.ds(0, halo), pl.ds(halo, own), pl.ds(halo + own, halo))[k]

    def clip_send(f, k):
        return pltpu.make_async_remote_copy(
            clip.at[f],
            xin.at[f, place(k)],
            k_send.at[f, k // 2],
            x_recv.at[f, k],
            device_id={"segment": seg, "band": band + 1 - k},
            device_id_type=MESH,
        )

    def x_copy(f, k):
        return pltpu.make_async_remote_copy(
            outs.at[f],
            xin.at[f, place(k)],
            x_send.at[f, k],
            x_recv.at[f, k],
            device_id={"segment": seg + 1, "band": band + 1 - k},
            device_id_type=MESH,
        )

    def both(side, fn_list):
        @pl.when(side)
        def _():
            for fn in fn_list:
                fn()

    seg0_down, seg0_up = jnp.logical_and(first, has_down), jnp.logical_and(first, has_up)
    both(seg0_down, [lambda: clip_send(0, 0).start()])
    both(seg0_up, [lambda: clip_send(0, 2).start()])
    for l in range(depth):
        both(has_down, [lambda l=l: cache_down(l).start()])
        both(has_up, [lambda l=l: cache_up(l).start()])
    both(seg0_down, [lambda: clip_send(1, 0).start()])
    both(seg0_up, [lambda: clip_send(1, 2).start()])

    sh[:, 0:PAD, :] = jnp.zeros((sh.shape[0], PAD, chan), jnp.float32)
    sh[:, PAD + width : 2 * PAD + width, :] = jnp.zeros((sh.shape[0], PAD, chan), jnp.float32)

    @pl.when(jnp.logical_not(has_up))
    def _():
        cext[:, :, 0:halo] = jnp.zeros((depth, 2, halo, width, chan), jnp.bfloat16)
        xin[:, 0:halo] = jnp.zeros((frames, halo, width, chan), jnp.bfloat16)

    @pl.when(jnp.logical_not(has_down))
    def _():
        cext[:, :, halo + own :] = jnp.zeros((depth, 2, halo, width, chan), jnp.bfloat16)
        xin[:, halo + own :] = jnp.zeros((frames, halo, width, chan), jnp.bfloat16)

    def put_shifted(dst, row, value):
        sh[row, PAD : PAD + width, :] = value
        dst[row, :, 0:chan] = sh[row, PAD - 1 : PAD - 1 + width, :].astype(jnp.bfloat16)
        dst[row, :, chan : 2 * chan] = value.astype(jnp.bfloat16)
        dst[row, :, 2 * chan : 3 * chan] = sh[row, PAD + 1 : PAD + 1 + width, :].astype(jnp.bfloat16)

    def patches(src, row):
        parts = [src[pl.ds(row - 1 + i, 2)].reshape(2 * width, 3 * chan) for i in range(3)]
        return jnp.concatenate(parts, axis=1)

    def taps(l, lo, hi):
        return wd[l, :, :, lo * chan : hi * chan].reshape(9 * chan, (hi - lo) * chan)

    def dot(a, b):
        return jnp.dot(a, b, preferred_element_type=jnp.float32)

    for l in range(depth):
        for t in range(3):
            w_copies[l][t].wait()
        cl_copies[l].wait()
        both(has_up, [lambda l=l: cache_down(l).wait_recv()])
        both(has_down, [lambda l=l: cache_up(l).wait_recv()])

        def spread(row, carry, l=l):
            for f in range(2):
                put_shifted(c3.at[f], row, cext[l, f, row].astype(jnp.float32))
            return carry

        lax.fori_loop(l, ext - l, spread, 0)

        def past(q, carry, l=l):
            row = l + 1 + 2 * q
            newer = dot(patches(c3.at[1], row), taps(l, 1, 3))
            older = dot(patches(c3.at[0], row), taps(l, 2, 3))
            bias = bias_ref[l]
            p0[l][pl.ds(2 * q, 2)] = (newer[:, :chan] + older + bias).reshape(2, width, chan)
            p1[l][pl.ds(2 * q, 2)] = (newer[:, chan:] + bias).reshape(2, width, chan)
            return carry

        lax.fori_loop(0, (own + 2 * (halo - 1 - l)) // 2, past, 0)

    def activate(dst, row, x):
        at = band * own + row - halo
        inside = jnp.logical_and(at >= 0, at < bands * own)
        act = x * (0.5 * jnp.tanh(0.5 * x) + 0.5)
        put_shifted(dst, row, jnp.where(inside, act, 0.0))

    for f in range(frames):
        if f == 0:
            @pl.when(first)
            def _():
                clip_copy.wait()

        @pl.when(jnp.logical_not(first))
        def _(f=f):
            x_copy(f, 1).wait_recv()

        both(has_up, [lambda f=f: x_copy(f, 0).wait_recv()])
        both(has_down, [lambda f=f: x_copy(f, 2).wait_recv()])

        def enter(row, carry, f=f):
            x = xin[f, row].astype(jnp.float32)
            xs[row] = x
            activate(a3.at[0], row, x)
            return carry

        lax.fori_loop(0, ext, enter, 0)
        for l in range(depth):

            def layer(q, carry, f=f, l=l):
                row = l + 1 + 2 * q
                src, dst = a3.at[l % 2], a3.at[(l + 1) % 2]
                if f == 0:
                    acc = dot(patches(src, row), taps(l, 0, 2))
                    own_sum = acc[:, :chan].reshape(2, width, chan) + p0[l][pl.ds(2 * q, 2)]
                    p1[l][pl.ds(2 * q, 2)] += acc[:, chan:].reshape(2, width, chan)
                else:
                    acc = dot(patches(src, row), taps(l, 0, 1))
                    own_sum = acc.reshape(2, width, chan) + p1[l][pl.ds(2 * q, 2)]
                x = xs[pl.ds(row, 2)] + live_ref[l] * own_sum
                if l < depth - 1:
                    xs[pl.ds(row, 2)] = x
                    for k in range(2):
                        activate(dst, row + k, x[k])
                else:
                    outs[f, pl.ds(row - halo, 2)] = x.astype(jnp.bfloat16)
                return carry

            lax.fori_loop(0, (own + 2 * (halo - 1 - l)) // 2, layer, 0)

        @pl.when(jnp.logical_not(last))
        def _(f=f):
            x_copy(f, 1).start()

        both(jnp.logical_and(jnp.logical_not(last), has_down), [lambda f=f: x_copy(f, 0).start()])
        both(jnp.logical_and(jnp.logical_not(last), has_up), [lambda f=f: x_copy(f, 2).start()])
        pltpu.make_async_copy(outs.at[f], out.at[0, f], out_sem.at[f]).start()

    for f in range(frames):
        pltpu.make_async_copy(outs.at[f], out.at[0, f], out_sem.at[f]).wait()

        @pl.when(jnp.logical_not(last))
        def _(f=f):
            x_copy(f, 1).wait_send()

        both(jnp.logical_and(jnp.logical_not(last), has_down), [lambda f=f: x_copy(f, 0).wait_send()])
        both(jnp.logical_and(jnp.logical_not(last), has_up), [lambda f=f: x_copy(f, 2).wait_send()])
        both(seg0_down, [lambda f=f: clip_send(f, 0).wait_send()])
        both(seg0_up, [lambda f=f: clip_send(f, 2).wait_send()])
    for l in range(depth):
        both(has_down, [lambda l=l: cache_down(l).wait_send()])
        both(has_up, [lambda l=l: cache_up(l).wait_send()])


def per_device(clip, caches, weights, biases, section_layers):
    segments, bands = lax.axis_size("segment"), lax.axis_size("band")
    frames, own, width, chan = clip.shape
    depth = weights.shape[1]
    halo = depth
    ext = own + 2 * halo
    live = (jnp.arange(depth) < section_layers[0]).astype(jnp.float32)
    live = jnp.broadcast_to(live[:, None, None], (depth, 1, chan))
    bias = biases[0][:, None, :]
    bf, f32 = jnp.bfloat16, jnp.float32
    sums = [pltpu.VMEM((own + 2 * (halo - 1 - l), width, chan), f32) for l in range(depth)]
    dma = pltpu.SemaphoreType.DMA
    dims = (segments, bands, frames, own, width, chan, depth)
    return pl.pallas_call(
        functools.partial(kernel, dims),
        out_shape=jax.ShapeDtypeStruct((1,) + clip.shape, bf),
        in_specs=[pl.BlockSpec(memory_space=pltpu.VMEM)] * 2 + [pl.BlockSpec(memory_space=pl.ANY)] * 3,
        out_specs=pl.BlockSpec(memory_space=pl.ANY),
        scratch_shapes=[
            pltpu.VMEM((depth, 9, chan, 3 * chan), bf),
            pltpu.VMEM((depth, 2, ext, width, chan), bf),
            pltpu.VMEM((2, ext, width, 3 * chan), bf),
            pltpu.VMEM((2, ext, width, 3 * chan), bf),
            pltpu.VMEM((ext, width + 2 * PAD, chan), f32),
            pltpu.VMEM((ext, width, chan), f32),
            pltpu.VMEM((frames, ext, width, chan), bf),
            pltpu.VMEM((frames, own, width, chan), bf),
            *sums,
            *sums,
            dma((depth, 3)),
            dma((depth,)),
            dma((depth, 2)),
            dma((depth, 2)),
            dma,
            dma((frames, 2)),
            dma((frames, 3)),
            dma((frames, 3)),
            dma((frames,)),
        ],
        compiler_params=pltpu.CompilerParams(
            collective_id=0, has_side_effects=True, vmem_limit_bytes=56 * 2**20
        ),
    )(live, bias, clip, caches, weights)


def solution(mesh):
    placed = (
        P(None, "band", None, None),
        P("segment", None, None, "band", None, None),
        P("segment", None, None, None, None, None),
        P("segment", None, None),
        P("segment"),
    )
    return jax.shard_map(
        per_device,
        mesh=mesh,
        in_specs=placed,
        out_specs=P("segment", None, "band", None, None),
        check_vma=False,
    )
```

```python
import functools

import jax
import jax.numpy as jnp
from jax import lax
from jax.experimental import pallas as pl
from jax.experimental.pallas import tpu as pltpu
from jax.sharding import PartitionSpec as P

MESH = pl.DeviceIdType.MESH
CHUNK = 2
PARTS = 2


def kernel(dims, count_ref, bias_ref, clip, caches, weights, out, *scratch):
    segments, bands, frames, own, width, chan, depth = dims
    wp, cext, c3, xs, xin, outs = scratch[:6]
    a3 = scratch[6 : 6 + depth]
    sums = scratch[6 + depth : 6 + 2 * depth]
    (w_sem, cl_sem, ch_send, ch_recv, cm_sem, f_send, f_recv, z_send, z_recv, out_sem) = scratch[6 + 2 * depth :]
    halo = depth
    ext = own + 2 * halo
    taps = 3 * 3
    f32, bf16 = jnp.float32, jnp.bfloat16
    seg = lax.axis_index("segment")
    band = lax.axis_index("band")
    first, last = seg == 0, seg == segments - 1
    inner, sender = jnp.logical_not(first), jnp.logical_not(last)
    has_up, has_down = band > 0, band < bands - 1

    def when(cond, *steps):
        @pl.when(cond)
        def _():
            for step in steps:
                step()

    def w_copy(l, t, k):
        return pltpu.make_async_copy(
            weights.at[0, l, :, t],
            wp.at[l, t, pl.ds(3 * k, taps), :, pl.ds(k * chan, chan)],
            w_sem.at[l, t, k],
        )

    def own_cache(l):
        return pltpu.make_async_copy(caches.at[0, l], cext.at[l, :, pl.ds(halo, own)], cl_sem.at[l])

    clip_copy = pltpu.make_async_copy(clip, xin.at[:, pl.ds(halo, own)], cm_sem)
    for l in range(depth):
        own_cache(l).start()
        for t in range(3):
            for k in range(2):
                w_copy(l, t, k).start()
    when(first, clip_copy.start)

    barrier = pltpu.get_barrier_semaphore()

    def greet(cond, ds, db):
        @pl.when(cond)
        def _():
            pl.semaphore_signal(
                barrier, inc=1, device_id={"segment": seg + ds, "band": band + db}, device_id_type=MESH
            )
        return cond.astype(jnp.int32)

    greeted = greet(has_up, 0, -1) + greet(has_down, 0, 1) + greet(inner, -1, 0) + greet(sender, 1, 0)
    pl.semaphore_wait(barrier, greeted)

    def remote(src, dst, send, recv, ds, db):
        return pltpu.make_async_remote_copy(
            src, dst, send, recv, device_id={"segment": seg + ds, "band": band + db}, device_id_type=MESH
        )

    sides = ((0, 1, has_down, has_up), (1, -1, has_up, has_down))

    def cache_halo(l, side):
        src = pl.ds(l, own - l) if side == 0 else pl.ds(0, own - l)
        dst = pl.ds(l, own - l) if side == 0 else pl.ds(halo + own, own - l)
        return remote(
            caches.at[0, l, :, src], cext.at[l, :, dst], ch_send.at[l, side], ch_recv.at[l, side], 0, 1 - 2 * side
        )

    def forward(f, c, side, source):
        src = clip.at[f, pl.ds(CHUNK * c, CHUNK)] if source else xin.at[f, pl.ds(halo + CHUNK * c, CHUNK)]
        dst = xin.at[f, pl.ds(CHUNK * c + (halo + own) * side, CHUNK)]
        return remote(src, dst, f_send.at[f, c, side], f_recv.at[f, c, side], 0, 1 - 2 * side)

    def relay(f, c):
        return remote(
            outs.at[f, pl.ds(CHUNK * c, CHUNK)],
            xin.at[f, pl.ds(halo + CHUNK * c, CHUNK)],
            z_send.at[f, c],
            z_recv.at[f, c],
            1,
            0,
        )

    def send_clip(f):
        for side, _, to, _ in sides:
            when(jnp.logical_and(first, to), *[forward(f, c, side, True).start for c in range(PARTS)])

    for l in range(depth):
        for side, _, to, _ in sides:
            when(to, cache_halo(l, side).start)
        if l == depth - 2:
            send_clip(0)
    send_clip(1)

    def clear(l, carry):
        for t in range(3):
            wp[l, t, taps : taps + 3, :, 0:chan] = jnp.zeros((3, chan, chan), bf16)
            wp[l, t, 0:3, :, chan : 2 * chan] = jnp.zeros((3, chan, chan), bf16)
        return carry

    lax.fori_loop(0, depth, clear, 0)

    @pl.when(jnp.logical_not(has_up))
    def _():
        cext[:, :, 0:halo] = jnp.zeros((depth, 2, halo, width, chan), bf16)
        xin[:, 0:halo] = jnp.zeros((frames, halo, width, chan), bf16)

    @pl.when(jnp.logical_not(has_down))
    def _():
        cext[:, :, halo + own :] = jnp.zeros((depth, 2, halo, width, chan), bf16)
        xin[:, halo + own :] = jnp.zeros((frames, halo, width, chan), bf16)

    column = lax.broadcasted_iota(jnp.int32, (width, chan), 0)
    at_left, at_right = column == 0, column == width - 1

    def put_shifted(dst, row, value):
        left = jnp.where(at_left, 0.0, pltpu.roll(value, 1, 0))
        right = jnp.where(at_right, 0.0, pltpu.roll(value, width - 1, 0))
        dst[row, :, 0:chan] = left.astype(bf16)
        dst[row, :, chan : 2 * chan] = value.astype(bf16)
        dst[row, :, 2 * chan : 3 * chan] = right.astype(bf16)

    def pair_dot(l, t, sources):
        lhs = jnp.concatenate([src[row + i] for src, row in sources for i in range(4)], axis=1)
        rhs = wp[l, t : t + len(sources)].reshape(len(sources) * (taps + 3) * chan, 2 * chan)
        return jnp.dot(lhs, rhs, preferred_element_type=f32)

    for l in range(depth):
        own_cache(l).wait()
        for side, _, _, has in sides:
            when(has, cache_halo(l, side).wait_recv)
        for row in range(ext - 2 * l):
            for f in range(2):
                put_shifted(c3.at[l % 2, f], row, cext[l, f, l + row].astype(f32))
        for t in range(2):
            for k in range(2):
                w_copy(l, t, k).wait()
        bias = bias_ref[0, l : l + 1]
        older, newer = c3.at[l % 2, 0], c3.at[l % 2, 1]
        for row in range(0, own + 2 * (halo - 1 - l), 2):
            now = pair_dot(l, 0, [(older, row), (newer, row)])
            later = pair_dot(l, 0, [(newer, row)])
            for k in range(2):
                sums[l][0, row + k] = now[:, k * chan : (k + 1) * chan] + bias
                sums[l][1, row + k] = later[:, k * chan : (k + 1) * chan] + bias
    for l in range(depth):
        for k in range(2):
            w_copy(l, 2, k).wait()

    def activate(l, row, x):
        act = x * (0.5 * jnp.tanh(0.5 * x) + 0.5)
        if row < halo:
            act = jnp.where(has_up, act, 0.0)
        if row >= halo + own:
            act = jnp.where(has_down, act, 0.0)
        put_shifted(a3[l], row - l, act)

    lives = [jnp.clip(count_ref[0] - l, 0, 1).astype(f32) for l in range(depth)]

    def frame(f, carry):
        when(jnp.logical_and(first, f == 0), clip_copy.wait)
        for c in range(PARTS):
            when(inner, relay(f, c).wait_recv)
            for side, _, to, _ in sides:
                when(jnp.logical_and(inner, to), forward(f, c, side, False).start)

        def enter(row):
            x = xin[f, row].astype(f32)
            xs[row] = x
            activate(0, row, x)

        for row in range(halo, halo + own):
            enter(row)
        for side, _, _, has in sides:
            when(has, *[forward(f, c, side, False).wait_recv for c in range(PARTS)])
        for row in [*range(halo), *range(halo + own, ext)]:
            enter(row)
        for l in range(depth):
            for pair in range(0, own + 2 * (halo - 1 - l), 2):
                acc = pair_dot(l, 2, [(a3[l], pair)])
                for k in range(2):
                    row = l + 1 + pair + k
                    add = acc[:, k * chan : (k + 1) * chan] + sums[l][f, pair + k]
                    x = xs[row] + lives[l] * add
                    if l < depth - 1:
                        xs[row] = x
                        activate(l + 1, row, x)
                    else:
                        outs[f, row - halo] = x.astype(bf16)
                if l == depth - 1:
                    when(sender, relay(f, pair // 2).start)
        pltpu.make_async_copy(outs.at[f], out.at[0, f], out_sem.at[f]).start()

        @pl.when(f == 0)
        def _():
            for l in range(depth):
                for pair in range(0, own + 2 * (halo - 1 - l), 2):
                    acc = pair_dot(l, 1, [(a3[l], pair)])
                    for k in range(2):
                        sums[l][1, pair + k] += acc[:, k * chan : (k + 1) * chan]

        return carry

    lax.fori_loop(0, frames, frame, 0)

    for f in range(frames):
        pltpu.make_async_copy(outs.at[f], out.at[0, f], out_sem.at[f]).wait()
        for c in range(PARTS):
            when(sender, relay(f, c).wait_send)
            for side, _, to, _ in sides:
                when(to, forward(f, c, side, False).wait_send)
    for l in range(depth):
        for side, _, to, _ in sides:
            when(to, cache_halo(l, side).wait_send)


def per_device(clip, caches, weights, biases, section_layers):
    segments, bands = lax.axis_size("segment"), lax.axis_size("band")
    frames, own, width, chan = clip.shape
    depth = weights.shape[1]
    halo = depth
    ext = own + 2 * halo
    bf, f32 = jnp.bfloat16, jnp.float32
    dma = pltpu.SemaphoreType.DMA
    dims = (segments, bands, frames, own, width, chan, depth)
    return pl.pallas_call(
        functools.partial(kernel, dims),
        out_shape=jax.ShapeDtypeStruct((1,) + clip.shape, bf),
        in_specs=[pl.BlockSpec(memory_space=pltpu.SMEM), pl.BlockSpec(memory_space=pltpu.VMEM)]
        + [pl.BlockSpec(memory_space=pl.ANY)] * 3,
        out_specs=pl.BlockSpec(memory_space=pl.ANY),
        scratch_shapes=[
            pltpu.VMEM((depth, 3, 12, chan, 2 * chan), bf),
            pltpu.VMEM((depth, 2, ext, width, chan), bf),
            pltpu.VMEM((2, 2, ext, width, 3 * chan), bf),
            pltpu.VMEM((ext, width, chan), f32),
            pltpu.VMEM((frames, ext, width, chan), bf),
            pltpu.VMEM((frames, own, width, chan), bf),
            *[pltpu.VMEM((ext - 2 * l, width, 3 * chan), bf) for l in range(depth)],
            *[pltpu.VMEM((frames, ext - 2 * l - 2, width, chan), f32) for l in range(depth)],
            dma((depth, 3, 2)),
            dma((depth,)),
            dma((depth, 2)),
            dma((depth, 2)),
            dma,
            dma((frames, PARTS, 2)),
            dma((frames, PARTS, 2)),
            dma((frames, PARTS)),
            dma((frames, PARTS)),
            dma((frames,)),
        ],
        compiler_params=pltpu.CompilerParams(
            collective_id=0, has_side_effects=True, vmem_limit_bytes=56 * 2**20
        ),
    )(section_layers, biases, clip, caches, weights)


def solution(mesh):
    placed = (
        P(None, "band", None, None),
        P("segment", None, None, "band", None, None),
        P("segment", None, None, None, None, None),
        P("segment", None, None),
        P("segment"),
    )
    return jax.shard_map(
        per_device,
        mesh=mesh,
        in_specs=placed,
        out_specs=P("segment", None, "band", None, None),
        check_vma=False,
    )
```

```python
import functools

import jax
import jax.numpy as jnp
from jax import lax
from jax.experimental import pallas as pl
from jax.experimental.pallas import tpu as pltpu
from jax.sharding import PartitionSpec as P

MESH = pl.DeviceIdType.MESH
CHUNK = 1
PARTS = 4
HALF = 2


def kernel(dims, count_ref, bias_ref, clip, caches, weights, out, *scratch):
    segments, bands, frames, own, width, chan, depth = dims
    wp, cext, xin, mid, outs = scratch[:5]
    c3 = scratch[5 : 5 + depth]
    a3 = scratch[5 + depth : 6 + 2 * depth]
    sums = scratch[6 + 2 * depth : 6 + 3 * depth]
    xs = scratch[6 + 3 * depth : 7 + 4 * depth]
    (w_sem, cl_sem, ch_send, ch_recv, cm_sem, h_send, h_recv, f_send, f_recv, z_send, z_recv, out_sem) = scratch[7 + 4 * depth :]
    halo = depth
    ext = own + 2 * halo
    taps = 3 * 3
    f32, bf16 = jnp.float32, jnp.bfloat16
    seg = lax.axis_index("segment")
    band = lax.axis_index("band")
    first, last = seg == 0, seg == segments - 1
    inner, sender = jnp.logical_not(first), jnp.logical_not(last)
    odd = lax.rem(band, 2)
    has_up, has_down = band > 0, band < bands - 1
    has_far = jnp.logical_or(jnp.logical_and(odd == 0, has_up), jnp.logical_and(odd == 1, has_down))
    near, far = 0, 1
    below = (1 - odd, odd)

    def when(cond, *steps):
        @pl.when(cond)
        def _():
            for step in steps:
                step()

    def exists(side, *steps):
        if side == near:
            for step in steps:
                step()
        else:
            when(has_far, *steps)

    def edge(side, n):
        return below[side] * (own - n)

    def landing(side, n):
        return below[side] * (halo - n) + (1 - below[side]) * (halo + own)

    def region(side, n):
        return (1 - below[side]) * (halo - n) + below[side] * (halo + own)

    def w_copy(l, t, k):
        return pltpu.make_async_copy(
            weights.at[0, l, :, t],
            wp.at[l, t, pl.ds(3 * k, taps), :, pl.ds(k * chan, chan)],
            w_sem.at[l, t, k],
        )

    def own_cache(l):
        return pltpu.make_async_copy(caches.at[0, l], cext.at[l, :, pl.ds(halo, own)], cl_sem.at[l])

    clip_copy = pltpu.make_async_copy(clip, xin.at[:, pl.ds(halo, own)], cm_sem)

    def load(l):
        for t in range(2):
            for k in range(2):
                w_copy(l, t, k).start()

    for l in range(2):
        own_cache(l).start()
        load(l)

    barrier = pltpu.get_barrier_semaphore()

    def greet(cond, ds, db):
        @pl.when(cond)
        def _():
            pl.semaphore_signal(
                barrier, inc=1, device_id={"segment": seg + ds, "band": band + db}, device_id_type=MESH
            )
        return cond.astype(jnp.int32)

    greeted = greet(has_up, 0, -1) + greet(has_down, 0, 1) + greet(inner, -1, 0) + greet(sender, 1, 0)
    pl.semaphore_wait(barrier, greeted)
    for l in range(2, depth):
        own_cache(l).start()
        load(l)
    when(first, clip_copy.start)
    for l in range(depth):
        for k in range(2):
            w_copy(l, 2, k).start()

    def remote(src, dst, send, recv, ds, db):
        return pltpu.make_async_remote_copy(
            src, dst, send, recv, device_id={"segment": seg + ds, "band": band + db}, device_id_type=MESH
        )

    def beside(src, dst, send, recv, side):
        return remote(src, dst, send, recv, 0, 2 * below[side] - 1)

    def cache_halo(l, n, side, arrived=False):
        src = caches.at[0, l, :, pl.ds(edge(side, n), n)]
        dst = cext.at[l, :, pl.ds(region(side, n) if arrived else landing(side, n), n)]
        return beside(src, dst, ch_send.at[l, side], ch_recv.at[l, side], side)

    def clip_halo(f, side, arrived=False):
        src = clip.at[f, pl.ds(edge(side, HALF), HALF)]
        dst = xin.at[f, pl.ds(region(side, HALF) if arrived else landing(side, HALF), HALF)]
        return beside(src, dst, h_send.at[f, 0, side], h_recv.at[f, 0, side], side)

    def mid_halo(f, side, arrived=False):
        src = mid.at[f, pl.ds(halo + edge(side, HALF), HALF)]
        dst = mid.at[f, pl.ds(region(side, HALF) if arrived else landing(side, HALF), HALF)]
        return beside(src, dst, h_send.at[f, 1, side], h_recv.at[f, 1, side], side)

    def forward(f, c, side, arrived=False):
        src = xin.at[f, pl.ds(halo + CHUNK * c, CHUNK)]
        dst = xin.at[f, pl.ds((region(side, halo) if arrived else landing(side, halo)) + CHUNK * c, CHUNK)]
        return beside(src, dst, f_send.at[f, c, side], f_recv.at[f, c, side], side)

    def relay(f, c):
        return remote(
            outs.at[f, pl.ds(CHUNK * c, CHUNK)],
            xin.at[f, pl.ds(halo + CHUNK * c, CHUNK)],
            z_send.at[f, c],
            z_recv.at[f, c],
            1,
            0,
        )

    depths = tuple(own - l for l in range(depth))
    halves = tuple(HALF - l % HALF for l in range(depth))

    def start_first():
        for side in (far, near):
            exists(side, *[cache_halo(l, halves[l], side).start for l in range(HALF)], clip_halo(0, side).start)
            exists(side, *[cache_halo(l, halves[l], side).start for l in range(HALF, depth)])
        for side in (far, near):
            exists(side, clip_halo(1, side).start)

    def start_inner():
        for l in range(depth):
            for side in (far, near):
                exists(side, cache_halo(l, depths[l], side).start)

    when(first, start_first)
    when(inner, start_inner)

    def clear(l, carry):
        for t in range(3):
            wp[l, t, taps : taps + 3, :, 0:chan] = jnp.zeros((3, chan, chan), bf16)
            wp[l, t, 0:3, :, chan : 2 * chan] = jnp.zeros((3, chan, chan), bf16)
        return carry

    lax.fori_loop(0, depth, clear, 0)

    @pl.when(jnp.logical_not(has_far))
    def _():
        rows = pl.ds(region(far, halo), halo)
        for f in range(2):
            xin[f, rows] = jnp.zeros((halo, width, chan), bf16)
            mid[f, rows] = jnp.zeros((halo, width, chan), bf16)
            for l in range(depth):
                cext[l, f, rows] = jnp.zeros((halo, width, chan), bf16)

    column = lax.broadcasted_iota(jnp.int32, (width, chan), 0)
    at_left, at_right = column == 0, column == width - 1

    def put_shifted(dst, row, value):
        left = jnp.where(at_left, 0.0, pltpu.roll(value, 1, 0))
        right = jnp.where(at_right, 0.0, pltpu.roll(value, width - 1, 0))
        dst[row, :, 0:chan] = left.astype(bf16)
        dst[row, :, chan : 2 * chan] = value.astype(bf16)
        dst[row, :, 2 * chan : 3 * chan] = right.astype(bf16)

    def pair_dot(l, t, sources, row):
        lhs = jnp.concatenate([src[row - 1 + i] for src in sources for i in range(4)], axis=1)
        rhs = wp[l, t : t + len(sources)].reshape(len(sources) * (taps + 3) * chan, 2 * chan)
        return jnp.dot(lhs, rhs, preferred_element_type=f32)

    def spread(l, start, n):
        def step(i, carry):
            for f in range(2):
                put_shifted(c3[l].at[f], start + i, cext[l, f, start + i].astype(f32))
            return carry

        lax.fori_loop(0, n, step, 0)

    def history(l, rows):
        bias = bias_ref[0, l : l + 1]
        older, newer = c3[l].at[0], c3[l].at[1]
        for row in rows:
            now = pair_dot(l, 0, [older, newer], row)
            later = pair_dot(l, 0, [newer], row)
            for k in range(2):
                sums[l][0, row + k] = now[:, k * chan : (k + 1) * chan] + bias
                sums[l][1, row + k] = later[:, k * chan : (k + 1) * chan] + bias

    def renew(l, rows):
        for row in rows:
            acc = pair_dot(l, 1, [acts(l, 0)], row)
            for k in range(2):
                sums[l][1, row + k] += acc[:, k * chan : (k + 1) * chan]

    def at(l, f):
        return depth if l == HALF and isinstance(f, int) and f == 1 else l

    def acts(l, f):
        return a3[at(l, f)]

    def activate(l, f, row, x, outside=None):
        act = x * (0.5 * jnp.tanh(0.5 * x) + 0.5)
        if outside is None:
            line = band * own + row - halo
            act = jnp.where(jnp.logical_and(line >= 0, line < bands * own), act, 0.0)
        elif outside:
            act = jnp.where(has_far, act, 0.0)
        put_shifted(acts(l, f), row, act)

    def far_row(parity, row):
        if parity is None:
            return None
        return row < halo if parity == 0 else row >= halo + own

    def enter(src, f, l, rows, parity=None):
        for row in rows:
            x = src[f, row].astype(f32)
            xs[at(l, f)][row] = x
            activate(l, f, row, x, far_row(parity, row))

    lives = [jnp.clip(count_ref[0] - l, 0, 1).astype(f32) for l in range(depth)]

    def layer(f, l, rows, keep=False, parity=None):
        for row in rows:
            acc = pair_dot(l, 2, [acts(l, f)], row)
            for k in range(2):
                add = acc[:, k * chan : (k + 1) * chan] + sums[l][f, row + k]
                x = xs[at(l, f)][row + k] + lives[l] * add
                if l < depth - 1:
                    xs[at(l + 1, f)][row + k] = x
                    activate(l + 1, f, row + k, x, far_row(parity, row + k))
                    if keep:
                        mid[f, row + k] = x.astype(bf16)
                else:
                    outs[f, row + k - halo] = x.astype(bf16)

    def finish(f):
        for c in range(PARTS):
            if CHUNK * c % 2 == 0:
                layer(f, depth - 1, [halo + CHUNK * c])
            if CHUNK * c % 2 or CHUNK > 1:
                for part in range(c - (CHUNK == 1), c + 1):
                    when(sender, relay(f, part).start)
        pltpu.make_async_copy(outs.at[f], out.at[0, f], out_sem.at[f]).start()

    def load_taps(l, times):
        for t in times:
            for k in range(2):
                w_copy(l, t, k).wait()

    middle = list(range(halo, halo + own))

    def beyond(side, n):
        return [region(side, n) + i for i in range(n)]

    def first_section(parity):
        odd = parity

        def beyond(side, n):
            at_top = (parity, 1 - parity)[side]
            return [(halo - n if at_top else halo + own) + i for i in range(n)]

        early = ([5 - 2 * odd, 7 - 2 * odd], [6 - 2 * odd])
        late = ([3 + 4 * odd], [4 + 2 * odd])
        both = ([3, 5, 7], [4, 6])
        for l in range(depth):
            own_cache(l).wait()
            cache_halo(l, halves[l], near, True).wait_recv()
            spread(l, halo, own)
            spread(l, beyond(near, halves[l])[0], halves[l])
            load_taps(l, (0, 1))
            history(l, early[l % HALF])
        clip_copy.wait()
        load_taps(0, (2,))

        def more(l):
            when(has_far, cache_halo(l, halves[l], far, True).wait_recv)
            spread(l, beyond(far, halves[l])[0], halves[l])
            history(l, late[l % HALF])
            if l > 0:
                load_taps(l, (2,))

        for stage in range(2):
            for f in range(frames):
                src, arrival = ((xin, clip_halo), (mid, mid_halo))[stage]
                l0, l1 = 2 * stage, 2 * stage + 1
                if f == 1:
                    renew(l0, both[0])
                    renew(l1, both[1])
                if stage == 0:
                    enter(src, f, l0, middle, parity)
                arrival(f, near, True).wait_recv()
                enter(src, f, l0, beyond(near, HALF), parity)
                layer(f, l0, early[0], parity=parity)
                if f == 0 and stage == 0:
                    more(l0)
                    more(l1)
                when(has_far, arrival(f, far, True).wait_recv)
                enter(src, f, l0, beyond(far, HALF), parity)
                layer(f, l0, late[0], parity=parity)
                if stage == 0:
                    layer(f, l1, both[1], True, parity)
                    for side in (far, near):
                        exists(side, mid_halo(f, side).start)
                else:
                    finish(f)
            if stage == 0:
                more(2)
                more(3)

    def inner_section():
        for l in range(depth):
            own_cache(l).wait()
            cache_halo(l, depths[l], near, True).wait_recv()
            when(has_far, cache_halo(l, depths[l], far, True).wait_recv)
            spread(l, l, ext - 2 * l)
            load_taps(l, (0, 1))
            history(l, range(l + 1, ext - 1 - l, 2))
        for l in range(depth):
            load_taps(l, (2,))

        def take(f):
            for c in range(PARTS):
                relay(f, c).wait_recv()
                for side in (far, near):
                    exists(side, forward(f, c, side).start)

        take(0)

        def rows_of(parity, f):
            outer = list(range(halo)), list(range(halo + own, ext))
            near_rows, far_rows = outer[1 - parity], outer[parity]
            first_rows = ([5, 7, 9], [6, 8], [7]), ([1, 3, 5], [2, 4], [3])
            last_rows = ([1, 3], [2, 4], [3, 5]), ([7, 9], [6, 8], [5, 7])
            enter(xin, f, 0, middle, parity)
            for c in range(PARTS):
                forward(f, c, near, True).wait_recv()
            enter(xin, f, 0, near_rows, parity)
            for l in range(depth - 1):
                layer(f, l, first_rows[parity][l], parity=parity)
            when(has_far, *[forward(f, c, far, True).wait_recv for c in range(PARTS)])
            enter(xin, f, 0, far_rows, parity)
            for l in range(depth - 1):
                layer(f, l, last_rows[parity][l], parity=parity)
            finish(f)

        def frame(f, carry):
            for parity in range(2):
                when(odd == parity, lambda parity=parity: rows_of(parity, f))

            @pl.when(f == 0)
            def _():
                take(1)
                for l in range(depth):
                    renew(l, range(l + 1, ext - 1 - l, 2))

            return carry

        lax.fori_loop(0, frames, frame, 0)
        for f in range(frames):
            for c in range(PARTS):
                for side in (far, near):
                    exists(side, forward(f, c, side).wait_send)
        for l in range(depth):
            for side in (far, near):
                exists(side, cache_halo(l, depths[l], side).wait_send)

    def end_first():
        for f in range(frames):
            for side in (far, near):
                exists(side, clip_halo(f, side).wait_send, mid_halo(f, side).wait_send)
        for l in range(depth):
            for side in (far, near):
                exists(side, cache_halo(l, halves[l], side).wait_send)

    for parity in range(2):
        when(jnp.logical_and(first, odd == parity), lambda parity=parity: first_section(parity))
    when(first, end_first)
    when(inner, inner_section)

    for f in range(frames):
        pltpu.make_async_copy(outs.at[f], out.at[0, f], out_sem.at[f]).wait()
        for c in range(PARTS):
            when(sender, relay(f, c).wait_send)


def per_device(clip, caches, weights, biases, section_layers):
    segments, bands = lax.axis_size("segment"), lax.axis_size("band")
    frames, own, width, chan = clip.shape
    depth = weights.shape[1]
    halo = depth
    ext = own + 2 * halo
    bf, f32 = jnp.bfloat16, jnp.float32
    dma = pltpu.SemaphoreType.DMA
    dims = (segments, bands, frames, own, width, chan, depth)
    return pl.pallas_call(
        functools.partial(kernel, dims),
        out_shape=jax.ShapeDtypeStruct((1,) + clip.shape, bf),
        in_specs=[pl.BlockSpec(memory_space=pltpu.SMEM), pl.BlockSpec(memory_space=pltpu.VMEM)]
        + [pl.BlockSpec(memory_space=pl.ANY)] * 3,
        out_specs=pl.BlockSpec(memory_space=pl.ANY),
        scratch_shapes=[
            pltpu.VMEM((depth, 3, 12, chan, 2 * chan), bf),
            pltpu.VMEM((depth, 2, ext, width, chan), bf),
            pltpu.VMEM((frames, ext, width, chan), bf),
            pltpu.VMEM((frames, ext, width, chan), bf),
            pltpu.VMEM((frames, own, width, chan), bf),
            *[pltpu.VMEM((2, ext, width, 3 * chan), bf)] * depth,
            *[pltpu.VMEM((ext, width, 3 * chan), bf)] * (depth + 1),
            *[pltpu.VMEM((frames, ext, width, chan), f32)] * depth,
            *[pltpu.VMEM((ext, width, chan), f32)] * (depth + 1),
            dma((depth, 3, 2)),
            dma((depth,)),
            dma((depth, 2)),
            dma((depth, 2)),
            dma,
            dma((frames, 2, 2)),
            dma((frames, 2, 2)),
            dma((frames, PARTS, 2)),
            dma((frames, PARTS, 2)),
            dma((frames, PARTS)),
            dma((frames, PARTS)),
            dma((frames,)),
        ],
        compiler_params=pltpu.CompilerParams(
            collective_id=0, has_side_effects=True, vmem_limit_bytes=56 * 2**20
        ),
    )(section_layers, biases, clip, caches, weights)


def solution(mesh):
    placed = (
        P(None, "band", None, None),
        P("segment", None, None, "band", None, None),
        P("segment", None, None, None, None, None),
        P("segment", None, None),
        P("segment"),
    )
    return jax.shard_map(
        per_device,
        mesh=mesh,
        in_specs=placed,
        out_specs=P("segment", None, "band", None, None),
        check_vma=False,
    )
```

```python
import functools

import jax
import jax.numpy as jnp
from jax import lax
from jax.experimental import pallas as pl
from jax.experimental.pallas import tpu as pltpu
from jax.sharding import PartitionSpec as P

MESH = pl.DeviceIdType.MESH
CHUNK = 1
PARTS = 4
HALF = 2


def kernel(dims, count_ref, bias_ref, clip, caches, weights, out, *scratch):
    segments, bands, frames, own, width, chan, depth = dims
    wp, cext, xin, mid, outs = scratch[:5]
    c3 = scratch[5 : 5 + depth]
    a3 = scratch[5 + depth : 6 + 2 * depth]
    sums = scratch[6 + 2 * depth : 6 + 3 * depth]
    xs = scratch[6 + 3 * depth : 7 + 4 * depth]
    (w_sem, cl_sem, ch_send, ch_recv, cm_sem, h_send, h_recv, f_send, f_recv, z_send, z_recv, out_sem) = scratch[7 + 4 * depth :]
    halo = depth
    ext = own + 2 * halo
    taps = 3 * 3
    f32, bf16 = jnp.float32, jnp.bfloat16
    seg = lax.axis_index("segment")
    band = lax.axis_index("band")
    first, last = seg == 0, seg == segments - 1
    inner, sender = jnp.logical_not(first), jnp.logical_not(last)
    odd = lax.rem(band, 2)
    has_up, has_down = band > 0, band < bands - 1
    has_far = jnp.logical_or(jnp.logical_and(odd == 0, has_up), jnp.logical_and(odd == 1, has_down))
    near, far = 0, 1
    below = (1 - odd, odd)

    def when(cond, *steps):
        @pl.when(cond)
        def _():
            for step in steps:
                step()

    def exists(side, *steps):
        if side == near:
            for step in steps:
                step()
        else:
            when(has_far, *steps)

    def edge(side, n):
        return below[side] * (own - n)

    def landing(side, n):
        return below[side] * (halo - n) + (1 - below[side]) * (halo + own)

    def region(side, n):
        return (1 - below[side]) * (halo - n) + below[side] * (halo + own)

    def w_copy(l, t, k):
        return pltpu.make_async_copy(
            weights.at[0, l, :, t],
            wp.at[l, t, pl.ds(3 * k, taps), :, pl.ds(k * chan, chan)],
            w_sem.at[l, t, k],
        )

    def own_cache(l):
        return pltpu.make_async_copy(caches.at[0, l], cext.at[l, :, pl.ds(halo, own)], cl_sem.at[l])

    clip_copy = pltpu.make_async_copy(clip, xin.at[:, pl.ds(halo, own)], cm_sem)

    def load(l):
        for t in range(2):
            for k in range(2):
                w_copy(l, t, k).start()

    for l in range(2):
        own_cache(l).start()
        load(l)

    barrier = pltpu.get_barrier_semaphore()

    def greet(cond, ds, db):
        @pl.when(cond)
        def _():
            pl.semaphore_signal(
                barrier, inc=1, device_id={"segment": seg + ds, "band": band + db}, device_id_type=MESH
            )
        return cond.astype(jnp.int32)

    greeted = greet(has_up, 0, -1) + greet(has_down, 0, 1) + greet(inner, -1, 0) + greet(sender, 1, 0)
    pl.semaphore_wait(barrier, greeted)
    for l in range(2, depth):
        own_cache(l).start()
        load(l)
    when(first, clip_copy.start)
    for l in range(depth):
        for k in range(2):
            w_copy(l, 2, k).start()

    def remote(src, dst, send, recv, ds, db):
        return pltpu.make_async_remote_copy(
            src, dst, send, recv, device_id={"segment": seg + ds, "band": band + db}, device_id_type=MESH
        )

    def beside(src, dst, send, recv, side):
        return remote(src, dst, send, recv, 0, 2 * below[side] - 1)

    def cache_halo(l, n, side, arrived=False):
        src = caches.at[0, l, :, pl.ds(edge(side, n), n)]
        dst = cext.at[l, :, pl.ds(region(side, n) if arrived else landing(side, n), n)]
        return beside(src, dst, ch_send.at[l, side], ch_recv.at[l, side], side)

    def clip_halo(f, side, arrived=False):
        src = clip.at[f, pl.ds(edge(side, HALF), HALF)]
        dst = xin.at[f, pl.ds(region(side, HALF) if arrived else landing(side, HALF), HALF)]
        return beside(src, dst, h_send.at[f, 0, side], h_recv.at[f, 0, side], side)

    def mid_halo(f, side, arrived=False):
        src = mid.at[f, pl.ds(halo + edge(side, HALF), HALF)]
        dst = mid.at[f, pl.ds(region(side, HALF) if arrived else landing(side, HALF), HALF)]
        return beside(src, dst, h_send.at[f, 1, side], h_recv.at[f, 1, side], side)

    def forward(f, c, side, arrived=False):
        src = xin.at[f, pl.ds(halo + CHUNK * c, CHUNK)]
        dst = xin.at[f, pl.ds((region(side, halo) if arrived else landing(side, halo)) + CHUNK * c, CHUNK)]
        return beside(src, dst, f_send.at[f, c, side], f_recv.at[f, c, side], side)

    def relay(f, c):
        return remote(
            outs.at[f, pl.ds(CHUNK * c, CHUNK)],
            xin.at[f, pl.ds(halo + CHUNK * c, CHUNK)],
            z_send.at[f, c],
            z_recv.at[f, c],
            1,
            0,
        )

    depths = tuple(own - l for l in range(depth))
    halves = tuple(HALF - l % HALF for l in range(depth))

    def start_first():
        for side in (far, near):
            exists(side, *[cache_halo(l, halves[l], side).start for l in range(HALF)], clip_halo(0, side).start)
            exists(side, *[cache_halo(l, halves[l], side).start for l in range(HALF, depth)])
        for side in (far, near):
            exists(side, clip_halo(1, side).start)

    def start_inner():
        for l in range(depth):
            for side in (far, near):
                exists(side, cache_halo(l, depths[l], side).start)

    when(first, start_first)
    when(inner, start_inner)

    def clear(l, carry):
        for t in range(3):
            wp[l, t, taps : taps + 3, :, 0:chan] = jnp.zeros((3, chan, chan), bf16)
            wp[l, t, 0:3, :, chan : 2 * chan] = jnp.zeros((3, chan, chan), bf16)
        return carry

    lax.fori_loop(0, depth, clear, 0)

    @pl.when(jnp.logical_not(has_far))
    def _():
        rows = pl.ds(region(far, halo), halo)
        for f in range(2):
            xin[f, rows] = jnp.zeros((halo, width, chan), bf16)
            mid[f, rows] = jnp.zeros((halo, width, chan), bf16)
            for l in range(depth):
                cext[l, f, rows] = jnp.zeros((halo, width, chan), bf16)

    column = lax.broadcasted_iota(jnp.int32, (width, chan), 0)
    at_left, at_right = column == 0, column == width - 1

    def put_shifted(dst, row, value):
        left = jnp.where(at_left, 0.0, pltpu.roll(value, 1, 0))
        right = jnp.where(at_right, 0.0, pltpu.roll(value, width - 1, 0))
        dst[row, :, 0:chan] = left.astype(bf16)
        dst[row, :, chan : 2 * chan] = value.astype(bf16)
        dst[row, :, 2 * chan : 3 * chan] = right.astype(bf16)

    def pair_dot(l, t, sources, row):
        lhs = jnp.concatenate([src[row - 1 + i] for src in sources for i in range(4)], axis=1)
        rhs = wp[l, t : t + len(sources)].reshape(len(sources) * (taps + 3) * chan, 2 * chan)
        return jnp.dot(lhs, rhs, preferred_element_type=f32)

    def spread(l, start, n):
        def step(i, carry):
            for f in range(2):
                put_shifted(c3[l].at[f], start + i, cext[l, f, start + i].astype(f32))
            return carry

        lax.fori_loop(0, n, step, 0)

    def history(l, rows):
        bias = bias_ref[0, l : l + 1]
        older, newer = c3[l].at[0], c3[l].at[1]
        for row in rows:
            now = pair_dot(l, 0, [older, newer], row)
            later = pair_dot(l, 0, [newer], row)
            for k in range(2):
                sums[l][0, row + k] = now[:, k * chan : (k + 1) * chan] + bias
                sums[l][1, row + k] = later[:, k * chan : (k + 1) * chan] + bias

    def renew(l, rows):
        for row in rows:
            acc = pair_dot(l, 1, [acts(l, 0)], row)
            for k in range(2):
                sums[l][1, row + k] += acc[:, k * chan : (k + 1) * chan]

    def at(l, f):
        return depth if l == HALF and isinstance(f, int) and f == 1 else l

    def acts(l, f):
        return a3[at(l, f)]

    def activate(l, f, row, x, outside=None):
        act = x * (0.5 * jnp.tanh(0.5 * x) + 0.5)
        if outside is None:
            line = band * own + row - halo
            act = jnp.where(jnp.logical_and(line >= 0, line < bands * own), act, 0.0)
        elif outside is not False:
            act = jnp.where(outside, act, 0.0)
        put_shifted(acts(l, f), row, act)

    def far_row(parity, row):
        if parity is None:
            return None
        if row < halo:
            return (has_up, False, has_up)[parity]
        if row >= halo + own:
            return (False, has_down, has_down)[parity]
        return False

    def enter(src, f, l, rows, parity=None):
        for row in rows:
            x = src[f, row].astype(f32)
            xs[at(l, f)][row] = x
            activate(l, f, row, x, far_row(parity, row))

    lives = [jnp.clip(count_ref[0] - l, 0, 1).astype(f32) for l in range(depth)]

    def layer(f, l, rows, keep=False, parity=None):
        for row in rows:
            acc = pair_dot(l, 2, [acts(l, f)], row)
            for k in range(2):
                add = acc[:, k * chan : (k + 1) * chan] + sums[l][f, row + k]
                x = xs[at(l, f)][row + k] + lives[l] * add
                if l < depth - 1:
                    xs[at(l + 1, f)][row + k] = x
                    activate(l + 1, f, row + k, x, far_row(parity, row + k))
                    if keep:
                        mid[f, row + k] = x.astype(bf16)
                else:
                    outs[f, row + k - halo] = x.astype(bf16)

    def finish(f):
        for c in range(PARTS):
            if CHUNK * c % 2 == 0:
                layer(f, depth - 1, [halo + CHUNK * c])
            if CHUNK * c % 2 or CHUNK > 1:
                for part in range(c - (CHUNK == 1), c + 1):
                    when(sender, relay(f, part).start)
        pltpu.make_async_copy(outs.at[f], out.at[0, f], out_sem.at[f]).start()

    def load_taps(l, times):
        for t in times:
            for k in range(2):
                w_copy(l, t, k).wait()

    middle = list(range(halo, halo + own))

    def beyond(side, n):
        return [region(side, n) + i for i in range(n)]

    def first_section(parity):
        odd = parity

        def beyond(side, n):
            at_top = (parity, 1 - parity)[side]
            return [(halo - n if at_top else halo + own) + i for i in range(n)]

        early = ([5 - 2 * odd, 7 - 2 * odd], [6 - 2 * odd])
        late = ([3 + 4 * odd], [4 + 2 * odd])
        both = ([3, 5, 7], [4, 6])
        for l in range(depth):
            own_cache(l).wait()
            cache_halo(l, halves[l], near, True).wait_recv()
            spread(l, halo, own)
            spread(l, beyond(near, halves[l])[0], halves[l])
            load_taps(l, (0, 1))
            history(l, early[l % HALF])
        clip_copy.wait()
        load_taps(0, (2,))

        def more(l):
            when(has_far, cache_halo(l, halves[l], far, True).wait_recv)
            spread(l, beyond(far, halves[l])[0], halves[l])
            history(l, late[l % HALF])
            if l > 0:
                load_taps(l, (2,))

        for stage in range(2):
            for f in range(frames):
                src, arrival = ((xin, clip_halo), (mid, mid_halo))[stage]
                l0, l1 = 2 * stage, 2 * stage + 1
                if f == 1:
                    renew(l0, both[0])
                    renew(l1, both[1])
                if stage == 0:
                    enter(src, f, l0, middle, parity)
                arrival(f, near, True).wait_recv()
                enter(src, f, l0, beyond(near, HALF), parity)
                layer(f, l0, early[0], parity=parity)
                if f == 0 and stage == 0:
                    more(l0)
                    more(l1)
                when(has_far, arrival(f, far, True).wait_recv)
                enter(src, f, l0, beyond(far, HALF), parity)
                layer(f, l0, late[0], parity=parity)
                if stage == 0:
                    layer(f, l1, both[1], True, parity)
                    for side in (far, near):
                        exists(side, mid_halo(f, side).start)
                else:
                    finish(f)
            if stage == 0:
                more(2)
                more(3)

    def inner_section():
        for l in range(depth):
            own_cache(l).wait()
            cache_halo(l, depths[l], near, True).wait_recv()
            when(has_far, cache_halo(l, depths[l], far, True).wait_recv)
            spread(l, l, ext - 2 * l)
            load_taps(l, (0, 1))
            rolled = 2 if l < 2 else 0

            def two(i, carry, l=l):
                history(l, [l + 1 + 4 * i, l + 3 + 4 * i])
                return carry

            lax.fori_loop(0, rolled, two, 0)
            history(l, range(l + 1 + 4 * rolled, ext - 1 - l, 2))
        for l in range(depth):
            load_taps(l, (2,))

        def take(f):
            for c in range(PARTS):
                relay(f, c).wait_recv()
                for side in (far, near):
                    exists(side, forward(f, c, side).start)

        take(0)

        def rows_of(parity, f):
            outer = list(range(halo)), list(range(halo + own, ext))
            near_rows, far_rows = outer[1 - parity], outer[parity]
            first_rows = ([5, 7, 9], [6, 8], [7]), ([1, 3, 5], [2, 4], [3])
            last_rows = ([1, 3], [2, 4], [3, 5]), ([7, 9], [6, 8], [5, 7])
            enter(xin, f, 0, middle, parity)
            for c in range(PARTS):
                forward(f, c, near, True).wait_recv()
            enter(xin, f, 0, near_rows, parity)
            for l in range(depth - 1):
                layer(f, l, first_rows[parity][l], parity=parity)
            when(has_far, *[forward(f, c, far, True).wait_recv for c in range(PARTS)])
            enter(xin, f, 0, far_rows, parity)
            for l in range(depth - 1):
                layer(f, l, last_rows[parity][l], parity=parity)
            finish(f)

        for parity in range(2):
            when(odd == parity, lambda parity=parity: rows_of(parity, 0))
        take(1)
        for l in range(depth):
            renew(l, range(l + 1, ext - 1 - l, 2))
        enter(xin, 1, 0, middle, 2)
        for c in range(PARTS):
            forward(1, c, near, True).wait_recv()
        when(has_far, *[forward(1, c, far, True).wait_recv for c in range(PARTS)])
        enter(xin, 1, 0, [*range(halo), *range(halo + own, ext)], 2)
        for l in range(depth - 1):
            layer(1, l, range(l + 1, ext - 1 - l, 2), parity=2)
        finish(1)
        for f in range(frames):
            for c in range(PARTS):
                for side in (far, near):
                    exists(side, forward(f, c, side).wait_send)
        for l in range(depth):
            for side in (far, near):
                exists(side, cache_halo(l, depths[l], side).wait_send)

    def end_first():
        for f in range(frames):
            for side in (far, near):
                exists(side, clip_halo(f, side).wait_send, mid_halo(f, side).wait_send)
        for l in range(depth):
            for side in (far, near):
                exists(side, cache_halo(l, halves[l], side).wait_send)

    for parity in range(2):
        when(jnp.logical_and(first, odd == parity), lambda parity=parity: first_section(parity))
    when(first, end_first)
    when(inner, inner_section)

    for f in range(frames):
        pltpu.make_async_copy(outs.at[f], out.at[0, f], out_sem.at[f]).wait()
        for c in range(PARTS):
            when(sender, relay(f, c).wait_send)


def per_device(clip, caches, weights, biases, section_layers):
    segments, bands = lax.axis_size("segment"), lax.axis_size("band")
    frames, own, width, chan = clip.shape
    depth = weights.shape[1]
    halo = depth
    ext = own + 2 * halo
    bf, f32 = jnp.bfloat16, jnp.float32
    dma = pltpu.SemaphoreType.DMA
    dims = (segments, bands, frames, own, width, chan, depth)
    return pl.pallas_call(
        functools.partial(kernel, dims),
        out_shape=jax.ShapeDtypeStruct((1,) + clip.shape, bf),
        in_specs=[pl.BlockSpec(memory_space=pltpu.SMEM), pl.BlockSpec(memory_space=pltpu.VMEM)]
        + [pl.BlockSpec(memory_space=pl.ANY)] * 3,
        out_specs=pl.BlockSpec(memory_space=pl.ANY),
        scratch_shapes=[
            pltpu.VMEM((depth, 3, 12, chan, 2 * chan), bf),
            pltpu.VMEM((depth, 2, ext, width, chan), bf),
            pltpu.VMEM((frames, ext, width, chan), bf),
            pltpu.VMEM((frames, ext, width, chan), bf),
            pltpu.VMEM((frames, own, width, chan), bf),
            *[pltpu.VMEM((2, ext, width, 3 * chan), bf)] * depth,
            *[pltpu.VMEM((ext, width, 3 * chan), bf)] * (depth + 1),
            *[pltpu.VMEM((frames, ext, width, chan), f32)] * depth,
            *[pltpu.VMEM((ext, width, chan), f32)] * (depth + 1),
            dma((depth, 3, 2)),
            dma((depth,)),
            dma((depth, 2)),
            dma((depth, 2)),
            dma,
            dma((frames, 2, 2)),
            dma((frames, 2, 2)),
            dma((frames, PARTS, 2)),
            dma((frames, PARTS, 2)),
            dma((frames, PARTS)),
            dma((frames, PARTS)),
            dma((frames,)),
        ],
        compiler_params=pltpu.CompilerParams(
            collective_id=0, has_side_effects=True, vmem_limit_bytes=56 * 2**20
        ),
    )(section_layers, biases, clip, caches, weights)


def solution(mesh):
    placed = (
        P(None, "band", None, None),
        P("segment", None, None, "band", None, None),
        P("segment", None, None, None, None, None),
        P("segment", None, None),
        P("segment"),
    )
    return jax.shard_map(
        per_device,
        mesh=mesh,
        in_specs=placed,
        out_specs=P("segment", None, "band", None, None),
        check_vma=False,
    )
```
